32 devices in a mesh: row: 8 (over z, y), col: 4 (over x, core).
Axes of the slice: x: 2, y: 2, z: 4, core: 2. Of those that a mesh axis runs over, the one named last changes fastest.
Arguments:
- tokens_in: bfloat16 [10240, 1024], P('row', 'col'), may hold values from -6 to 6
- grad_out: bfloat16 [10240, 1024], P('row', 'col'), may hold values from -6 to 6
- keep_mask: int32 [32, 256], P('row'), may hold values 0 or 1
- adapter_index: int32 [32], P('row'), may hold values from 0 to 7
- ln_gain: float32 [2, 1024], replicated, may hold values from 0.25 to 1.75
- ln_shift: float32 [2, 1024], replicated, may hold values from -1.8 to 1.8
- w_qkv: bfloat16 [3, 1024, 1024], P(None, 'row', 'col'), may hold values from -0.1875 to 0.1875
- bias_qv: bfloat16 [2, 1024], P(None, 'col'), may hold values from -1.796875 to 1.796875
- w_proj: bfloat16 [1024, 1024], P('col', 'row'), may hold values from -1.5 to 1.5
- w_fc1: bfloat16 [1024, 4096], P('row', 'col'), may hold values from -0.1875 to 0.1875
- bias_fc1: bfloat16 [4096], P('col'), may hold values from -1.796875 to 1.796875
- w_fc2: bfloat16 [4096, 1024], P('col', 'row'), may hold values from -0.09375 to 0.09375
- bias_out: bfloat16 [2, 1024], replicated, may hold values from -1.796875 to 1.796875
- qkv_down: bfloat16 [8, 16, 1024], replicated, may hold values from -0.1875 to 0.1875
- qkv_up: bfloat16 [8, 16, 3, 1024], replicated, may hold values from -0.75 to 0.75
- proj_down: bfloat16 [8, 16, 1024], replicated, may hold values from -1.5 to 1.5
- proj_up: bfloat16 [8, 16, 1024], replicated, may hold values from -0.75 to 0.75
- fc1_down: bfloat16 [8, 16, 1024], replicated, may hold values from -0.1875 to 0.1875
- fc1_up: bfloat16 [8, 16, 4096], replicated, may hold values from -0.75 to 0.75
- fc2_down: bfloat16 [8, 16, 4096], replicated, may hold values from -0.09375 to 0.09375
- fc2_up: bfloat16 [8, 16, 1024], replicated, may hold values from -0.75 to 0.75
Outputs:
- layer_out: bfloat16 [10240, 1024], P('row', 'col')
- grad_in: bfloat16 [10240, 1024], P('row', 'col')
- grad_qkv_down: float32 [8, 16, 1024], replicated
- grad_qkv_up: float32 [8, 16, 3, 1024], replicated
- grad_proj_down: float32 [8, 16, 1024], replicated
- grad_proj_up: float32 [8, 16, 1024], replicated
- grad_fc1_down: float32 [8, 16, 1024], replicated
- grad_fc1_up: float32 [8, 16, 4096], replicated
- grad_fc2_down: float32 [8, 16, 4096], replicated
- grad_fc2_up: float32 [8, 16, 1024], replicated
The draws below stay inside these ranges and needn't reach their ends.
All inputs are finite; a program needn't handle non-finite values. No bound on the sum of `keep_mask` on one device may be relied on, other than what follows from the above.
Results may differ from the reference program's by a relative error of at most 0.013.
Values may be sent and summed in bfloat16 or wider, within the bound.
No kernel may reach another device: no remote copies, remote signals or barrier semaphores. Data moves between devices by JAX's collectives and lax.ppermute only.
A program may use at most 192 MiB of HBM per device.

```python
import jax
import jax.numpy as jnp
from jax import lax

D = 1024
H = 16
HD = 64
FF = 4096
BUF = 64
SLOTS = 256
R = 16
NA = 8
IMG_ROW = 4
SEQ = 320
IMAGES = 32
TOKENS = 10240
N_ROW = 8


def plant(entries, key, smallest, top_value):
    longest = entries.shape.index(max(entries.shape))
    spots = []
    for shift in (0, 1):
        where = [jax.random.randint(jax.random.fold_in(key, axis), (), 0, length) for axis, length in enumerate(entries.shape)]
        where[longest] = (where[longest] + shift) % entries.shape[longest]
        spots.append(tuple(where))
    return entries.at[spots[0]].set(smallest).at[spots[1]].set(top_value)


def block_levels(own_key, extent, cuts, smallest, top_value):
    def one(axis_at, shards_of):
        heights = jax.random.uniform(jax.random.fold_in(jax.random.fold_in(own_key, 6), axis_at), (shards_of,), jnp.float32, smallest / len(cuts), top_value / len(cuts))
        return jnp.repeat(jnp.exp(heights), extent[axis_at] // shards_of).reshape((-1,) + (1,) * (len(extent) - axis_at - 1))

    factor_of = one(*cuts[0])
    for cut in cuts[1:]:
        factor_of = factor_of * one(*cut)
    return factor_of


def bell_draw(own_key, shape, spread, most, shards=(), held_as=jnp.bfloat16):
    gain = block_levels(own_key, shape, shards, -0.22, 0.18) if shards else 1.0
    entries = jax.random.normal(own_key, shape, jnp.float32) * spread * gain
    return jnp.minimum(jnp.maximum(entries, -most), most).astype(held_as)


def setup_inputs(seed: int = 0) -> dict:
    splits = jax.random.split(jax.random.key(seed), 22)
    return {
        "tokens_in": bell_draw(splits[0], (TOKENS, D), 1.0, 6.0, ((0, 8), (1, 4))),
        "grad_out": bell_draw(splits[1], (TOKENS, D), 1.0, 6.0, ((0, 8), (1, 4))),
        "keep_mask": plant((jax.random.randint(splits[2], (IMAGES, SLOTS), 0, 3) < 1).astype(jnp.int32), jax.random.fold_in(splits[2], 1), 0, 1),
        "adapter_index": plant(jax.random.randint(splits[3], (IMAGES,), 0, NA), jax.random.fold_in(splits[3], 1), 0, NA - 1).astype(jnp.int32),
        "ln_gain": jnp.clip(1.0 + 0.15 * jax.random.normal(splits[4], (2, D), jnp.float32), 0.25, 1.75),
        "ln_shift": bell_draw(splits[5], (2, D), 0.3, 1.8, (), jnp.float32),
        "w_qkv": bell_draw(splits[6], (3, D, D), D ** -0.5, 0.1875, ((1, 8), (2, 4))),
        "bias_qv": bell_draw(splits[7], (2, D), 0.3, 1.796875, ((1, 4),)),
        "w_proj": bell_draw(splits[8], (D, D), (max(D // 64, 1)) ** -0.5, 1.5, ((0, 4), (1, 8))),
        "w_fc1": bell_draw(splits[9], (D, FF), D ** -0.5, 0.1875, ((0, 8), (1, 4))),
        "bias_fc1": bell_draw(splits[10], (FF,), 0.3, 1.796875, ((0, 4),)),
        "w_fc2": bell_draw(splits[11], (FF, D), FF ** -0.5, 0.09375, ((0, 4), (1, 8))),
        "bias_out": bell_draw(splits[12], (2, D), 0.3, 1.796875),
        "qkv_down": bell_draw(splits[13], (NA, R, D), D ** -0.5, 0.1875),
        "qkv_up": bell_draw(splits[14], (NA, R, 3, D), (4 * R) ** -0.5, 0.75),
        "proj_down": bell_draw(splits[15], (NA, R, D), (max(D // 64, 1)) ** -0.5, 1.5),
        "proj_up": bell_draw(splits[16], (NA, R, D), (4 * R) ** -0.5, 0.75),
        "fc1_down": bell_draw(splits[17], (NA, R, D), D ** -0.5, 0.1875),
        "fc1_up": bell_draw(splits[18], (NA, R, FF), (4 * R) ** -0.5, 0.75),
        "fc2_down": bell_draw(splits[19], (NA, R, FF), FF ** -0.5, 0.09375),
        "fc2_up": bell_draw(splits[20], (NA, R, D), (4 * R) ** -0.5, 0.75),
    }


highest = lax.Precision.HIGHEST

@jax.custom_vjp
def low(v):
    return lax.optimization_barrier(v.astype(jnp.bfloat16)).astype(jnp.float32)

@jax.custom_vjp
def low_back(v):
    return v

def low_keep(v):
    return (low(v), None)

def low_pass(kept, grad):
    return (grad,)

def back_keep(v):
    return (v, None)

def back_low(kept, grad):
    return (low(grad),)
low.defvjp(low_keep, low_pass)
low_back.defvjp(back_keep, back_low)

def matmul(left_side, right_side):
    return jnp.dot(left_side, right_side, precision=highest, preferred_element_type=jnp.float32)

def normalize(values, gain_row, shift_row):
    row_mean = lax.optimization_barrier(jnp.mean(values, axis=-1, keepdims=True))
    centered = values - row_mean
    variance = lax.optimization_barrier(jnp.mean(centered * centered, axis=-1, keepdims=True))
    return centered * lax.rsqrt(variance + 1e-06) * gain_row + shift_row

def adapted(inputs, weight, down_map, up_map, select):
    latent = matmul(inputs, down_map.reshape(NA * R, -1).T) * select
    return matmul(inputs, weight) + matmul(latent, up_map.reshape(NA * R, -1))

def encoder_layer(hidden, qkv_down, qkv_up, proj_down, proj_up, fc1_down, fc1_up, fc2_down, fc2_up, frozen, keep_rows, select, key_open):
    ln_gain, ln_shift, w_qkv, bias_qv, w_proj, w_fc1, bias_fc1, w_fc2, bias_out = frozen
    images = key_open.shape[0]
    normed_one = low(normalize(hidden, ln_gain[0], ln_shift[0]))
    projected = [adapted(normed_one, w_qkv[section], qkv_down, qkv_up[:, :, section, :], select) for section in range(3)]
    queries = low(low_back(projected[0] + bias_qv[0]))
    key_side = low(low_back(projected[1]))
    value_side = low(low_back(projected[2] + bias_qv[1]))
    head_shape = (images, SEQ, H, HD)
    scores = jnp.einsum('gqhd,gkhd->ghqk', queries.reshape(head_shape), key_side.reshape(head_shape), precision=highest) * 0.125
    scores = low_back(scores)
    scores = jnp.where(key_open[:, None, None, :], scores, -1e+30)
    top_score = lax.optimization_barrier(jnp.max(scores, axis=-1, keepdims=True))
    exponent = jnp.exp(scores - top_score)
    soft_low = low(exponent / lax.optimization_barrier(jnp.sum(exponent, axis=-1, keepdims=True)))
    attended = jnp.einsum('ghqk,gkhd->gqhd', soft_low, value_side.reshape(head_shape), precision=highest)
    attended = low(low_back(attended.reshape(images * SEQ, D)))
    branch = low_back(adapted(attended, w_proj, proj_down, proj_up, select) + bias_out[0])
    middle = hidden + branch
    normed_two = low(normalize(middle, ln_gain[1], ln_shift[1]))
    pre_gelu = low_back(adapted(normed_two, w_fc1, fc1_down, fc1_up, select) + bias_fc1)
    activated = low(jax.nn.gelu(pre_gelu, approximate=False))
    result = low_back(adapted(activated, w_fc2, fc2_down, fc2_up, select) + bias_out[1])
    return keep_rows * (middle + result)

def reference(tokens_in, grad_out, keep_mask, adapter_index, ln_gain, ln_shift, w_qkv, bias_qv, w_proj, w_fc1, bias_fc1, w_fc2, bias_out, qkv_down, qkv_up, proj_down, proj_up, fc1_down, fc1_up, fc2_down, fc2_up):
    group_count = 1
    while group_count * 2 <= N_ROW and IMG_ROW * SEQ * group_count * 2 <= 4096:
        group_count = group_count * 2
    per_step = IMG_ROW * group_count
    step_count = IMAGES // per_step
    frozen = (ln_gain.astype(jnp.float32), ln_shift.astype(jnp.float32), w_qkv.astype(jnp.float32), bias_qv.astype(jnp.float32), w_proj.astype(jnp.float32), w_fc1.astype(jnp.float32), bias_fc1.astype(jnp.float32), w_fc2.astype(jnp.float32), bias_out.astype(jnp.float32))
    adapters = tuple((matrix.astype(jnp.float32) for matrix in (qkv_down, qkv_up, proj_down, proj_up, fc1_down, fc1_up, fc2_down, fc2_up)))
    inputs_all = tokens_in.reshape(step_count, per_step * SEQ, D)
    grads_all = grad_out.reshape(step_count, per_step * SEQ, D)
    keeps_all = keep_mask.reshape(step_count, per_step, SLOTS)
    owners_all = adapter_index.reshape(step_count, per_step)
    column_ids = jnp.arange(NA * R, dtype=jnp.int32) // R

    def one_step(totals, sliced):
        block_in, block_grad, block_keep, block_owner = sliced
        keep_full = jnp.concatenate([jnp.ones((per_step, BUF), jnp.int32), block_keep], axis=1)
        key_open = keep_full > 0
        keep_rows = keep_full.reshape(per_step * SEQ, 1).astype(jnp.float32)
        owner_rows = jnp.broadcast_to(block_owner[:, None], (per_step, SEQ)).reshape(per_step * SEQ, 1)
        select = (owner_rows == column_ids[None, :]).astype(jnp.float32)

        def forward(hidden, *weights):
            return encoder_layer(hidden, *weights, frozen, keep_rows, select, key_open)
        layer_out, pullback = jax.vjp(forward, block_in.astype(jnp.float32), *adapters)
        cotangents = pullback(block_grad.astype(jnp.float32))
        totals = tuple((running + addend for running, addend in zip(totals, cotangents[1:])))
        return (totals, (layer_out.astype(jnp.bfloat16), cotangents[0].astype(jnp.bfloat16)))
    initial = tuple((jnp.zeros_like(matrix) for matrix in adapters))
    totals, (outs_all, grads_in) = lax.scan(one_step, initial, (inputs_all, grads_all, keeps_all, owners_all))
    return (outs_all.reshape(TOKENS, D), grads_in.reshape(TOKENS, D), totals[0], totals[1], totals[2], totals[3], totals[4], totals[5], totals[6], totals[7])
```

```python
import jax
import jax.numpy as jnp
from jax import lax
from jax.experimental import pallas as pl
from jax.experimental.pallas import tpu as pltpu
from jax.sharding import PartitionSpec as P

D = 1024
H = 16
HD = 64
FF = 4096
BUF = 64
R = 16
NA = 8
SEQ = 320
PAIR = 2 * HD
PAIRS = H // 2
LANES = 128
CHUNKS = FF // D


BF = jnp.bfloat16
F32 = jnp.float32
ANY = pl.BlockSpec(memory_space=pl.ANY)
AXES = ("row", "col")


def nn(left, right):
    return lax.dot_general(left, right, (((1,), (0,)), ((), ())), preferred_element_type=F32)


def nt(left, right):
    return lax.dot_general(left, right, (((1,), (1,)), ((), ())), preferred_element_type=F32)


def tn(left, right):
    return lax.dot_general(left, right, (((0,), (0,)), ((), ())), preferred_element_type=F32)


def norm_parts(values):
    row_mean = jnp.mean(values, axis=-1, keepdims=True)
    centered = values - row_mean
    variance = jnp.mean(centered * centered, axis=-1, keepdims=True)
    inverse = lax.rsqrt(variance + 1e-06)
    return centered * inverse, inverse


def norm_back(grad_normed, gain_row, unit_rows, inverse):
    scaled = grad_normed * gain_row
    first_mean = jnp.mean(scaled, axis=-1, keepdims=True)
    second_mean = jnp.mean(scaled * unit_rows, axis=-1, keepdims=True)
    return inverse * (scaled - first_mean - unit_rows * second_mean)


def wide(ref):
    return jnp.concatenate([ref[i] for i in range(ref.shape[0])], axis=-1)


def head_mask(which):
    lanes = lax.broadcasted_iota(jnp.int32, (SEQ, PAIR), 1)
    return (lanes >= HD) if which else (lanes < HD)


def start_copy(source, target, sem):
    pltpu.make_async_copy(source, target, sem).start()


def copy_early(scalars, sources, w_early, sems):
    if len(sources) == 1:
        for s in range(4):
            start_copy(sources[0].at[s], w_early.at[s], sems.at[s])
        return
    z, y, x, core = scalars[1], scalars[2], scalars[3], scalars[4]
    for which, source in enumerate(sources):
        half, far, other = (which // 2) % 2, which % 2, which // 4

        def one(slot, carry, source=source, half=half, far=far, other=other):
            near = slot // 4
            z_at = lax.rem(z - lax.rem(slot, 4) + 4, 4)
            x_step, y_step = (near, far) if half == 0 else (far, near)
            x_at = jnp.where(x_step == 1, 1 - x, x)
            y_at = jnp.where(y_step == 1, 1 - y, y)
            c_at = (1 - core) if other else core
            row_at = (z_at * 2 + y_at) * 128
            col_at = (x_at * 2 + c_at) * 256
            for piece in range(4):
                block = half * 4 + piece
                part = source.at[slot, pl.ds(piece * 128, 128), :]
                if block < 6:
                    target = w_early.at[
                        block // 2,
                        pl.ds(pl.multiple_of(row_at, 128), 128),
                        pl.ds(pl.multiple_of(col_at + (block % 2) * 128, 128), 128),
                    ]
                    start_copy(part, target, sems.at[block // 2])
                else:
                    target = w_early.at[
                        3,
                        pl.ds(pl.multiple_of(col_at + (block - 6) * 128, 128), 128),
                        pl.ds(pl.multiple_of(row_at, 128), 128),
                    ]
                    start_copy(part, target, sems.at[3])
            return carry

        lax.fori_loop(0, 8, one, 0)


def wait_full(ref, sem):
    pltpu.make_async_copy(ref, ref, sem).wait()


def front_body(count, scalars, *refs):
    sources = refs[:count]
    (
        x_ref,
        open_row,
        ln_gain,
        ln_shift,
        bias_qv,
        bias_out,
        qkv_down,
        qkv_up,
        proj_down,
        proj_up,
        qkv_out,
        attended_out,
        middle_out,
        normed_two_out,
        w_early,
        sems,
    ) = refs[count:]
    copy_early(scalars, sources, w_early, sems)
    hidden = wide(x_ref).astype(F32)
    unit_one, _ = norm_parts(hidden)
    normed_one = (unit_one * ln_gain[0:1, :] + ln_shift[0:1, :]).astype(BF)
    latent_one = nt(normed_one, qkv_down[0]).astype(BF)
    for s in range(3):
        wait_full(w_early.at[s], sems.at[s])
        part = nn(normed_one, w_early[s]) + nn(latent_one, qkv_up[0, s])
        if s == 0:
            part = part + bias_qv[0:1, :].astype(F32)
        if s == 2:
            part = part + bias_qv[1:2, :].astype(F32)
        part = part.astype(BF)
        for p in range(PAIRS):
            qkv_out[s, p] = part[:, p * PAIR : (p + 1) * PAIR]
    is_open = open_row[...] > 0

    def one_pair(p, carry):
        q, k, v = qkv_out[0, p], qkv_out[1, p], qkv_out[2, p]
        total = jnp.zeros((SEQ, PAIR), F32)
        for which in range(2):
            mine = head_mask(which)
            q_one = jnp.where(mine, q, jnp.zeros_like(q))
            v_one = jnp.where(mine, v, jnp.zeros_like(v))
            scores = nt(q_one, k) * 0.125
            scores = jnp.where(is_open, scores, -1e30)
            top = jnp.max(scores, axis=-1, keepdims=True)
            exponent = jnp.exp(scores - top)
            low = (exponent * (1.0 / jnp.sum(exponent, axis=-1, keepdims=True))).astype(BF)
            total = total + nn(low, v_one)
        attended_out[p] = total.astype(BF)
        return carry

    lax.fori_loop(0, PAIRS, one_pair, 0)
    attended = wide(attended_out)
    latent_two = nt(attended, proj_down[0]).astype(BF)
    wait_full(w_early.at[3], sems.at[3])
    branch = nn(attended, w_early[3]) + nn(latent_two, proj_up[0]) + bias_out[0:1, :].astype(F32)
    middle = wide(x_ref).astype(F32) + branch
    middle_out[...] = middle
    unit_two, _ = norm_parts(middle)
    normed_two_out[...] = (unit_two * ln_gain[1:2, :] + ln_shift[1:2, :]).astype(BF)


def copy_late(sources, w_one, w_two, sems):
    if len(sources) == 2:
        for c in range(CHUNKS):
            start_copy(sources[0].at[:, pl.ds(c * D, D)], w_one.at[c], sems.at[0, c])
            start_copy(sources[1].at[pl.ds(c * D, D), :], w_two.at[c], sems.at[1, c])
        return
    source = sources[0]
    for c in range(CHUNKS):

        def one(r, carry, c=c):
            device = r * CHUNKS + c
            row_at = pl.multiple_of(r * 128, 128)
            for h in range(8):
                start_copy(
                    source.at[device, pl.ds(h * 128, 128), :],
                    w_one.at[c, pl.ds(row_at, 128), pl.ds(h * 128, 128)],
                    sems.at[0, c],
                )
            start_copy(
                source.at[device, pl.ds(D, D), :],
                w_two.at[c, :, pl.ds(row_at, 128)],
                sems.at[1, c],
            )
            return carry

        lax.fori_loop(0, 8, one, 0)


def feed_body(count, scalars, *refs):
    sources = refs[:count]
    (
        g_ref,
        keep_col,
        middle_ref,
        normed_two,
        bias_fc1,
        bias_out,
        fc1_down,
        fc1_up,
        fc2_down,
        fc2_up,
        out_ref,
        grad_normed_out,
        grads_out,
        w_one,
        w_two,
        result_acc,
        latent_acc,
        grad_latent_acc,
        grad_latent_turned,
        latent_turned,
        sems,
    ) = refs[count:]
    copy_late(sources, w_one, w_two, sems)
    n_two = normed_two[...]
    keep = keep_col[...]
    grad_low = (wide(g_ref).astype(F32) * keep).astype(BF)
    latent_three = nt(n_two, fc1_down[0]).astype(BF)
    turned_three = nt(fc1_down[0], n_two).astype(BF)
    grad_latent_four = nt(grad_low, fc2_up[0]).astype(BF)
    turned_four = nt(fc2_up[0], grad_low).astype(BF)
    result_acc[...] = jnp.zeros_like(result_acc)
    grad_normed_out[...] = jnp.zeros_like(grad_normed_out)
    latent_acc[...] = jnp.zeros_like(latent_acc)
    latent_turned[...] = jnp.zeros_like(latent_turned)
    grad_latent_acc[...] = jnp.zeros_like(grad_latent_acc)
    grad_latent_turned[...] = jnp.zeros_like(grad_latent_turned)

    def one_chunk(c, carry):
        wait_full(w_one.at[c], sems.at[0, c])
        wait_full(w_two.at[c], sems.at[1, c])
        span = pl.ds(pl.multiple_of(c * D, D), D)
        up_one = fc1_up[0, :, span]
        down_two = fc2_down[0, :, span]
        pre = (
            nn(n_two, w_one[c]) + nn(latent_three, up_one) + bias_fc1[:, span].astype(F32)
        )
        cumulative = 0.5 * (1.0 + lax.erf(pre * 0.7071067811865476))
        activated = (pre * cumulative).astype(BF)
        slope = cumulative + pre * jnp.exp(-0.5 * pre * pre) * 0.3989422804014327
        grad_act = nt(grad_low, w_two[c]) + nn(grad_latent_four, down_two)
        grad_pre = (grad_act * slope).astype(BF)
        result_acc[...] += nn(activated, w_two[c])
        grad_normed_out[...] += nt(grad_pre, w_one[c])
        latent_acc[...] += nt(activated, down_two)
        latent_turned[...] += nt(down_two, activated)
        grad_latent_acc[...] += nt(grad_pre, up_one)
        grad_latent_turned[...] += nt(up_one, grad_pre)
        grads_out[:, pl.ds(pl.multiple_of(D + c * D, D), D)] = nn(turned_three, grad_pre).astype(BF)
        grads_out[:, pl.ds(pl.multiple_of(D + FF + c * D, D), D)] = nn(
            turned_four, activated
        ).astype(BF)
        return carry

    lax.fori_loop(0, CHUNKS, one_chunk, 0)
    result = (
        result_acc[...]
        + nn(latent_acc[...].astype(BF), fc2_up[0])
        + bias_out[1:2, :].astype(F32)
    )
    out_rows = (keep * (middle_ref[...] + result)).astype(BF)
    width = out_ref.shape[2]
    for i in range(out_ref.shape[0]):
        out_ref[i] = out_rows[:, i * width : (i + 1) * width]
    grad_normed_out[...] += nn(grad_latent_acc[...].astype(BF), fc1_down[0])
    grads_out[:, 0:D] = nn(grad_latent_turned[...].astype(BF), n_two).astype(BF)
    grads_out[:, D + 2 * FF :] = nn(latent_turned[...].astype(BF), grad_low).astype(BF)


def back_body(count, scalars, *refs):
    sources = refs[:count]
    (
        x_ref,
        g_ref,
        keep_col,
        open_col,
        middle_ref,
        grad_normed_two,
        qkv_ref,
        attended_ref,
        ln_gain,
        ln_shift,
        qkv_down,
        qkv_up,
        proj_down,
        proj_up,
        grad_in_out,
        grads_up,
        grads_rest,
        w_early,
        grad_middle,
        grad_heads,
        grad_qkv,
        sems,
    ) = refs[count:]
    copy_early(scalars, sources, w_early, sems)
    unit_two, inverse_two = norm_parts(middle_ref[...])
    total = wide(g_ref).astype(F32) * keep_col[...] + norm_back(
        grad_normed_two[...], ln_gain[1:2, :], unit_two, inverse_two
    )
    grad_middle[...] = total
    grad_branch = total.astype(BF)
    attended = wide(attended_ref)
    grad_latent_two = nt(grad_branch, proj_up[0]).astype(BF)
    turned_grad_two = nt(proj_up[0], grad_branch).astype(BF)
    turned_two = nt(proj_down[0], attended).astype(BF)
    grads_rest[:, D : 2 * D] = nn(turned_grad_two, attended).astype(BF)
    grads_rest[:, 2 * D : 3 * D] = nn(turned_two, grad_branch).astype(BF)
    wait_full(w_early.at[3], sems.at[3])
    grad_attended = (nt(grad_branch, w_early[3]) + nn(grad_latent_two, proj_down[0])).astype(BF)
    for p in range(PAIRS):
        grad_heads[p] = grad_attended[:, p * PAIR : (p + 1) * PAIR]
    is_open = open_col[...] > 0

    def one_pair(p, carry):
        q, k, v, g = qkv_ref[0, p], qkv_ref[1, p], qkv_ref[2, p], grad_heads[p]
        zero = jnp.zeros_like(q)
        grad_q = jnp.zeros((SEQ, PAIR), F32)
        grad_k = jnp.zeros((SEQ, PAIR), F32)
        grad_v = jnp.zeros((SEQ, PAIR), F32)
        for which in range(2):
            mine = head_mask(which)
            q_one = jnp.where(mine, q, zero)
            k_one = jnp.where(mine, k, zero)
            v_one = jnp.where(mine, v, zero)
            g_one = jnp.where(mine, g, zero)
            scores = nt(k, q_one) * 0.125
            scores = jnp.where(is_open, scores, -1e30)
            top = jnp.max(scores, axis=0, keepdims=True)
            exponent = jnp.exp(scores - top)
            soft = exponent * (1.0 / jnp.sum(exponent, axis=0, keepdims=True))
            grad_v = grad_v + nn(soft.astype(BF), g_one)
            grad_soft = nt(v_one, g)
            inner = jnp.sum(grad_soft * soft, axis=0, keepdims=True)
            grad_scores = (soft * (grad_soft - inner)).astype(BF)
            grad_k = grad_k + nn(grad_scores, q_one)
            grad_q = grad_q + tn(grad_scores, k_one)
        grad_qkv[0, p] = (grad_q * 0.125).astype(BF)
        grad_qkv[1, p] = (grad_k * 0.125).astype(BF)
        grad_qkv[2, p] = grad_v.astype(BF)
        return carry

    lax.fori_loop(0, PAIRS, one_pair, 0)
    hidden = wide(x_ref).astype(F32)
    unit_one, inverse_one = norm_parts(hidden)
    normed_one = (unit_one * ln_gain[0:1, :] + ln_shift[0:1, :]).astype(BF)
    turned_one = nt(qkv_down[0], normed_one).astype(BF)
    grad_normed = jnp.zeros((SEQ, D), F32)
    latent = jnp.zeros((SEQ, R), F32)
    turned = jnp.zeros((R, SEQ), F32)
    for s in range(3):
        wait_full(w_early.at[s], sems.at[s])
        grad_part = wide(grad_qkv.at[s])
        grad_normed = grad_normed + nt(grad_part, w_early[s])
        latent = latent + nt(grad_part, qkv_up[0, s])
        turned = turned + nt(qkv_up[0, s], grad_part)
        grads_up[:, s * D : (s + 1) * D] = nn(turned_one, grad_part).astype(BF)
    grad_normed = grad_normed + nn(latent.astype(BF), qkv_down[0])
    grads_rest[:, 0:D] = nn(turned.astype(BF), normed_one).astype(BF)
    grad_rows = (
        grad_middle[...] + norm_back(grad_normed, ln_gain[0:1, :], unit_one, inverse_one)
    ).astype(BF)
    width = grad_in_out.shape[2]
    for i in range(grad_in_out.shape[0]):
        grad_in_out[i] = grad_rows[:, i * width : (i + 1) * width]


def sum_body(count, plan, owners, *refs):
    sources, outs = refs[:count], refs[count:]
    step = pl.program_id(0)
    for out, (first, steps) in zip(outs, plan):

        @pl.when((step >= first) & (step < first + steps))
        def _(out=out):
            flat = len(out.shape) == 3
            out[...] = jnp.zeros_like(out)
            at = 0
            for source in sources:

                def one(i, carry, source=source, at=at):
                    owner = owners[at + i]
                    addend = source[i].astype(F32)
                    if flat:
                        out[owner] += addend
                    else:
                        out[owner, 0] += addend
                    return carry

                lax.fori_loop(0, source.shape[0], one, 0)
                at += source.shape[0]


def adapter_sums(owners, sources, plan):
    steps = sum(entry[1] for entry in plan)
    out_specs, out_shapes = [], []
    for first, blocks, ups in plan:
        if ups:
            out_specs.append(
                pl.BlockSpec(
                    (NA, 1, R, D),
                    lambda i, o, first=first, blocks=blocks: (
                        0,
                        jnp.clip(i - first, 0, blocks - 1),
                        0,
                        0,
                    ),
                )
            )
            out_shapes.append(jax.ShapeDtypeStruct((NA, blocks, R, D), F32))
        else:
            out_specs.append(
                pl.BlockSpec(
                    (NA, R, D),
                    lambda i, o, first=first, blocks=blocks: (
                        0,
                        0,
                        jnp.clip(i - first, 0, blocks - 1),
                    ),
                )
            )
            out_shapes.append(jax.ShapeDtypeStruct((NA, R, blocks * D), F32))
    in_specs = [
        pl.BlockSpec((source.shape[0], R, D), lambda i, o: (0, 0, i)) for source in sources
    ]
    body = lambda owners_ref, *refs: sum_body(
        len(sources), [entry[:2] for entry in plan], owners_ref, *refs
    )
    return pl.pallas_call(
        body,
        grid_spec=pltpu.PrefetchScalarGridSpec(
            num_scalar_prefetch=1, grid=(steps,), in_specs=in_specs, out_specs=out_specs
        ),
        out_shape=out_shapes,
        name="adapter_sums",
    )(owners, *sources)


class Slice:
    def __init__(self):
        row, column = lax.axis_index("row"), lax.axis_index("col")
        self.z, self.y = row // 2, row % 2
        self.x, self.core = column // 2, column % 2

    @staticmethod
    def send(values, move):
        pairs = []
        for z in range(4):
            for y in range(2):
                for x in range(2):
                    for core in range(2):
                        to = move(z, y, x, core)
                        source = (z * 2 + y) * 4 + x * 2 + core
                        pairs.append((source, (to[0] * 2 + to[1]) * 4 + to[2] * 2 + to[3]))
        return lax.ppermute(values, AXES, pairs)

    def gather(self, both):
        up = lambda z, y, x, core: ((z + 1) % 4, y, x, core)
        over_x = lambda z, y, x, core: (z, y, 1 - x, core)
        over_y = lambda z, y, x, core: (z, 1 - y, x, core)
        over_core = lambda z, y, x, core: (z, y, x, 1 - core)
        line = [both]
        for _ in range(3):
            line.append(self.send(line[-1], up))
        mine = []
        for half in range(2):
            first, second = (over_x, over_y) if half == 0 else (over_y, over_x)
            four = jnp.stack([entry[half] for entry in line])
            eight = jnp.concatenate([four, self.send(four, first)])
            mine.append((eight, self.send(eight, second)))
        flat = [mine[0][0], mine[0][1], mine[1][0], mine[1][1]]
        return flat + [self.send(entry, over_core) for entry in flat]

    def owners(self, owners_all):
        rows = []
        slot = jnp.arange(8)
        for which in range(8):
            half, far, other = (which // 2) % 2, which % 2, which // 4
            near = slot // 4
            z_at = (self.z - slot % 4 + 4) % 4
            x_step, y_step = (near, far) if half == 0 else (far, near)
            x_at = jnp.where(x_step == 1, 1 - self.x, self.x)
            y_at = jnp.where(y_step == 1, 1 - self.y, self.y)
            c_at = (1 - self.core) if other else self.core
            rows.append(((z_at * 2 + y_at) * 4 + x_at * 2 + c_at))
        return [jnp.take(owners_all, jnp.concatenate([rows[h], rows[h + 1], rows[h + 4], rows[h + 5]])) for h in (0, 2)]


def side_by_side(block):
    rows, width = block.shape
    return jnp.concatenate(
        [block[:, i : i + LANES] for i in range(0, width, LANES)], axis=0
    )


def own_kernel(body, scalars, sources, operands, adapters, out_shapes, scratch, name):
    adapter_specs = [
        pl.BlockSpec(
            (1,) + entry.shape[1:], lambda i, s, n=entry.ndim: (s[0],) + (0,) * (n - 1)
        )
        for entry in adapters
    ]
    whole = lambda entry: pl.BlockSpec(entry.shape, lambda i, s, n=len(entry.shape): (0,) * n)
    return pl.pallas_call(
        lambda scalars_ref, *refs: body(len(sources), scalars_ref, *refs),
        grid_spec=pltpu.PrefetchScalarGridSpec(
            num_scalar_prefetch=1,
            grid=(1,),
            in_specs=[ANY] * len(sources) + [whole(entry) for entry in operands] + adapter_specs,
            out_specs=[whole(entry) for entry in out_shapes],
            scratch_shapes=scratch,
        ),
        out_shape=out_shapes,
        compiler_params=pltpu.CompilerParams(vmem_limit_bytes=60 * 1024 * 1024),
        name=name,
    )(scalars, *sources, *operands, *adapters)


def per_device(
    tokens_in,
    grad_out,
    keep_mask,
    adapter_index,
    ln_gain,
    ln_shift,
    w_qkv,
    bias_qv,
    w_proj,
    w_fc1,
    bias_fc1,
    w_fc2,
    bias_out,
    qkv_down,
    qkv_up,
    proj_down,
    proj_up,
    fc1_down,
    fc1_up,
    fc2_down,
    fc2_up,
):
    rows, columns = lax.axis_size("row"), lax.axis_size("col")
    column = lax.axis_index("col")
    images = adapter_index.shape[0]
    assert images == columns
    width = D // columns
    tuned = rows == 8 and columns == 4

    mine = lax.dynamic_slice_in_dim(keep_mask, column, 1, 0)
    open_row = jnp.concatenate([jnp.ones((1, BUF), jnp.int32), mine], axis=1).astype(F32)
    keep_col = open_row.reshape(SEQ, 1)
    adapter = lax.dynamic_slice_in_dim(adapter_index, column, 1, 0)
    owners_all = lax.all_gather(adapter_index, "row", axis=0, tiled=True)

    if tuned:
        place = Slice()
        late = lax.all_gather(
            jnp.concatenate([side_by_side(w_fc1), w_fc2], axis=0), AXES, axis=0, tiled=False
        )
        late_sources = [late]
        early_own = jnp.concatenate(
            [side_by_side(w_qkv[0]), side_by_side(w_qkv[1]), side_by_side(w_qkv[2])]
            + [w_proj],
            axis=0,
        )
        early_sources = place.gather(early_own.reshape(2, 512, LANES))
        scalars = jnp.concatenate(
            [adapter, jnp.stack([place.z, place.y, place.x, place.core]).astype(jnp.int32)]
        )
    else:
        scalars = jnp.concatenate([adapter, jnp.zeros((4,), jnp.int32)])
        qkv_full = lax.all_gather(
            lax.all_gather(w_qkv, "row", axis=1, tiled=True), "col", axis=2, tiled=True
        )
        proj_full = lax.all_gather(
            lax.all_gather(w_proj, "row", axis=1, tiled=True), "col", axis=0, tiled=True
        )
        early_sources = [jnp.concatenate([qkv_full, proj_full[None]], axis=0)]
        late_sources = [
            lax.all_gather(
                lax.all_gather(w_fc1, "row", axis=0, tiled=True), "col", axis=1, tiled=True
            ),
            lax.all_gather(
                lax.all_gather(w_fc2, "row", axis=1, tiled=True), "col", axis=0, tiled=True
            ),
        ]
    bias_qv_full = lax.all_gather(bias_qv, "col", axis=1, tiled=True)
    bias_fc1_full = lax.all_gather(bias_fc1, "col", axis=0, tiled=True).reshape(1, FF)

    def swap(values):
        return lax.all_to_all(values, "col", split_axis=0, concat_axis=0, tiled=True)

    x_blocks = swap(tokens_in.reshape(columns, SEQ, width))
    g_blocks = swap(grad_out.reshape(columns, SEQ, width))
    ups = jnp.transpose(qkv_up, (0, 2, 1, 3))

    shape = jax.ShapeDtypeStruct
    early_scratch = [pltpu.VMEM((4, D, D), BF)]
    qkv, attended, middle, normed_two = own_kernel(
        front_body,
        scalars,
        early_sources,
        [x_blocks, open_row, ln_gain, ln_shift, bias_qv_full, bias_out],
        [qkv_down, ups, proj_down, proj_up],
        [
            shape((3, PAIRS, SEQ, PAIR), BF),
            shape((PAIRS, SEQ, PAIR), BF),
            shape((SEQ, D), F32),
            shape((SEQ, D), BF),
        ],
        early_scratch + [pltpu.SemaphoreType.DMA((4,))],
        "front",
    )
    out_blocks, grad_normed_two, late_grads = own_kernel(
        feed_body,
        scalars,
        late_sources,
        [g_blocks, keep_col, middle, normed_two, bias_fc1_full, bias_out],
        [fc1_down, fc1_up, fc2_down, fc2_up],
        [
            shape((columns, SEQ, width), BF),
            shape((SEQ, D), F32),
            shape((R, 2 * D + 2 * FF), BF),
        ],
        [
            pltpu.VMEM((CHUNKS, D, D), BF),
            pltpu.VMEM((CHUNKS, D, D), BF),
            pltpu.VMEM((SEQ, D), F32),
            pltpu.VMEM((SEQ, R), F32),
            pltpu.VMEM((SEQ, R), F32),
            pltpu.VMEM((R, SEQ), F32),
            pltpu.VMEM((R, SEQ), F32),
            pltpu.SemaphoreType.DMA((2, CHUNKS)),
        ],
        "feed",
    )
    late_all = lax.all_gather(late_grads, AXES, axis=0, tiled=False)
    layer_out = swap(out_blocks).reshape(images * SEQ, width)
    grad_blocks, grads_up, grads_rest = own_kernel(
        back_body,
        scalars,
        early_sources,
        [
            x_blocks,
            g_blocks,
            keep_col,
            keep_col,
            middle,
            grad_normed_two,
            qkv,
            attended,
            ln_gain,
            ln_shift,
        ],
        [qkv_down, ups, proj_down, proj_up],
        [
            shape((columns, SEQ, width), BF),
            shape((R, 3 * D), BF),
            shape((R, 3 * D), BF),
        ],
        early_scratch
        + [
            pltpu.VMEM((SEQ, D), F32),
            pltpu.VMEM((PAIRS, SEQ, PAIR), BF),
            pltpu.VMEM((3, PAIRS, SEQ, PAIR), BF),
            pltpu.SemaphoreType.DMA((4,)),
        ],
        "back",
    )
    if tuned:
        parts = place.gather(jnp.stack([grads_up, grads_rest]))
        up_owners, rest_owners = place.owners(owners_all)
        up_parts = [parts[0], parts[1], parts[4], parts[5]]
        rest_parts = [parts[2], parts[3], parts[6], parts[7]]
    else:
        up_parts = [lax.all_gather(grads_up, AXES, axis=0, tiled=False)]
        rest_parts = [lax.all_gather(grads_rest, AXES, axis=0, tiled=False)]
        up_owners = rest_owners = owners_all
    grad_in = swap(grad_blocks).reshape(images * SEQ, width)
    blocks = FF // D
    g_fc1_down, g_fc1_up, g_fc2_down, g_fc2_up = adapter_sums(
        owners_all,
        [late_all],
        [(0, 1, False), (1, blocks, False), (1 + blocks, blocks, False), (1 + 2 * blocks, 1, False)],
    )
    (g_qkv_up,) = adapter_sums(up_owners, up_parts, [(0, 3, True)])
    g_qkv_down, g_proj_down, g_proj_up = adapter_sums(
        rest_owners, rest_parts, [(0, 1, False), (1, 1, False), (2, 1, False)]
    )
    return (
        layer_out,
        grad_in,
        g_qkv_down,
        jnp.transpose(g_qkv_up, (0, 2, 1, 3)),
        g_proj_down,
        g_proj_up,
        g_fc1_down,
        g_fc1_up,
        g_fc2_down,
        g_fc2_up,
    )


def solution(mesh):
    return jax.shard_map(
        per_device,
        mesh=mesh,
        in_specs=(
            P("row", "col"),
            P("row", "col"),
            P("row", None),
            P("row"),
            P(),
            P(),
            P(None, "row", "col"),
            P(None, "col"),
            P("col", "row"),
            P("row", "col"),
            P("col"),
            P("col", "row"),
            P(),
            P(),
            P(),
            P(),
            P(),
            P(),
            P(),
            P(),
            P(),
        ),
        out_specs=(P("row", "col"), P("row", "col"), P(), P(), P(), P(), P(), P(), P(), P()),
        check_vma=False,
    )
```
